256 devices in a mesh: seq: 64 (over z, y, core), dp: 4 (over x).
Axes of the slice: x: 4, y: 4, z: 8, core: 2. Of those that a mesh axis runs over, the one named last changes fastest.
Arguments:
- signal: bfloat16 [4, 65536, 384], P('dp', 'seq'), may hold values from -6 to 6
- filter_raw: bfloat16 [65536, 384], P('seq'), may hold values from -6 to 6
- cotangent: bfloat16 [4, 65536, 384], P('dp', 'seq'), may hold values from -6 to 6
- block_mask: int32 [4, 64], P('dp', 'seq'), may hold values from 0 to 1, as said below
Outputs:
- conv_out: bfloat16 [4, 65536, 384], P('dp', 'seq')
- signal_grad: bfloat16 [4, 65536, 384], P('dp', 'seq')
- filter_grad: bfloat16 [65536, 384], P('seq')
The draws below stay inside these ranges and needn't reach their ends.
Inputs may be any that keep to these rules, and one draw needn't show every extreme that they name: `block_mask`: each sequence's row is 1 on a leading run of blocks and 0 on the rest; every row has both.
All inputs are finite; a program needn't handle non-finite values.
Results may differ from the reference program's by a relative error of at most 0.013.
Values may be sent and summed in bfloat16 or wider, within the bound.
A program may use at most 128 MiB of HBM per device.

```python
import math
import jax
import jax.numpy as jnp
from jax import lax

CH = 384
BLK = 1024
RAD = 32
SEQ = 65536
RB = 64
NB = 128
BATCH = 4


def draw_block_mask(key, part):
    counts = jax.random.randint(key, (BATCH,), RB // 2, RB)
    return (jnp.arange(RB)[None, :] < counts[:, None]).astype(jnp.int32)


def steps_of(stream_key, extent, shards, smallest, largest):
    def one(position, shards_of):
        steps = jax.random.uniform(jax.random.fold_in(jax.random.fold_in(stream_key, 6), position), (shards_of,), jnp.float32, smallest / len(shards), largest / len(shards))
        return jnp.repeat(jnp.exp(steps), extent[position] // shards_of).reshape((-1,) + (1,) * (len(extent) - position - 1))

    gain = one(*shards[0])
    for cut in shards[1:]:
        gain = gain * one(*cut)
    return gain


def noise(key, dims, spread, bound, pieces=(), kind=jnp.bfloat16):
    level = steps_of(key, dims, pieces, -0.22, 0.18) if pieces else 1.0
    array = jax.random.normal(key, dims, jnp.float32) * spread * level
    return jnp.minimum(jnp.maximum(array, -bound), bound).astype(kind)


def setup_inputs(seed: int = 0) -> dict:
    streams_of = jax.random.split(jax.random.key(seed), 5)
    return {
        "signal": noise(streams_of[0], (BATCH, SEQ, CH), 1.0, 6.0, ((0, 4), (1, 64))),
        "filter_raw": noise(streams_of[1], (SEQ, CH), 1.0, 6.0, ((0, 64),)),
        "cotangent": noise(streams_of[2], (BATCH, SEQ, CH), 1.0, 6.0, ((0, 4), (1, 64))),
        "block_mask": draw_block_mask(jax.random.fold_in(streams_of[4], 71), 0),
    }


def angle_table(row_ids, col_ids, period):
    product = row_ids[:, None] * col_ids[None, :] % period
    return 2.0 * math.pi / period * product.astype(jnp.float32)

def rounded(values):
    return lax.optimization_barrier(values.astype(jnp.bfloat16)).astype(jnp.float32)

def table_pair(angles):
    return (jnp.cos(angles).astype(jnp.bfloat16).astype(jnp.float32), jnp.sin(angles).astype(jnp.bfloat16).astype(jnp.float32))

def make_tables():
    freq_ids = jnp.arange(NB, dtype=jnp.int32)
    block_ids = jnp.arange(RB, dtype=jnp.int32)
    column_ids = jnp.arange(BLK, dtype=jnp.int32)
    radix_ids = jnp.arange(RAD, dtype=jnp.int32)
    cos_one, sin_one = table_pair(angle_table(freq_ids, block_ids, NB))
    cos_rad, sin_rad = table_pair(angle_table(radix_ids, radix_ids, RAD))
    twist = angle_table(freq_ids, column_ids, NB * BLK)
    inner_twist = angle_table(radix_ids, radix_ids, BLK)
    return (cos_one, sin_one, cos_rad, sin_rad, jnp.cos(twist), jnp.sin(twist), jnp.cos(inner_twist), jnp.sin(inner_twist))

def forward_transform(values, tables):
    cos_one, sin_one, cos_rad, sin_rad, twist_cos, twist_sin, inner_cos, inner_sin = tables
    count = values.shape[0]
    data_rows = values.astype(jnp.float32)
    first_real = jnp.einsum('ka,nab->nkb', cos_one, data_rows)
    first_imag = -jnp.einsum('ka,nab->nkb', sin_one, data_rows)
    turned_real = rounded(first_real * twist_cos + first_imag * twist_sin).reshape(count, NB, RAD, RAD)
    turned_imag = rounded(first_imag * twist_cos - first_real * twist_sin).reshape(count, NB, RAD, RAD)
    mid_real = jnp.einsum('pr,nkpq->nkrq', cos_rad, turned_real) + jnp.einsum('pr,nkpq->nkrq', sin_rad, turned_imag)
    mid_imag = jnp.einsum('pr,nkpq->nkrq', cos_rad, turned_imag) - jnp.einsum('pr,nkpq->nkrq', sin_rad, turned_real)
    spun_real = rounded(mid_real * inner_cos + mid_imag * inner_sin)
    spun_imag = rounded(mid_imag * inner_cos - mid_real * inner_sin)
    last_real = jnp.einsum('qs,nkrq->nksr', cos_rad, spun_real) + jnp.einsum('qs,nkrq->nksr', sin_rad, spun_imag)
    last_imag = jnp.einsum('qs,nkrq->nksr', cos_rad, spun_imag) - jnp.einsum('qs,nkrq->nksr', sin_rad, spun_real)
    return (last_real.reshape(count, NB, BLK), last_imag.reshape(count, NB, BLK))

def inverse_transform(spec_real, spec_imag, factor, tables):
    cos_one, sin_one, cos_rad, sin_rad, twist_cos, twist_sin, inner_cos, inner_sin = tables
    count = spec_real.shape[0]
    round_real = rounded(spec_real).reshape(count, NB, RAD, RAD)
    round_imag = rounded(spec_imag).reshape(count, NB, RAD, RAD)
    mid_real = jnp.einsum('sq,nksr->nkrq', cos_rad, round_real) - jnp.einsum('sq,nksr->nkrq', sin_rad, round_imag)
    mid_imag = jnp.einsum('sq,nksr->nkrq', cos_rad, round_imag) + jnp.einsum('sq,nksr->nkrq', sin_rad, round_real)
    spun_real = rounded(mid_real * inner_cos - mid_imag * inner_sin)
    spun_imag = rounded(mid_imag * inner_cos + mid_real * inner_sin)
    back_real = jnp.einsum('rp,nkrq->nkpq', cos_rad, spun_real) - jnp.einsum('rp,nkrq->nkpq', sin_rad, spun_imag)
    back_imag = jnp.einsum('rp,nkrq->nkpq', cos_rad, spun_imag) + jnp.einsum('rp,nkrq->nkpq', sin_rad, spun_real)
    back_real = back_real.reshape(count, NB, BLK)
    back_imag = back_imag.reshape(count, NB, BLK)
    turned_real = rounded(back_real * twist_cos - back_imag * twist_sin)
    turned_imag = rounded(back_imag * twist_cos + back_real * twist_sin)
    combined = jnp.einsum('ka,nkb->nab', cos_one, turned_real) - jnp.einsum('ka,nkb->nab', sin_one, turned_imag)
    return (combined * factor).astype(jnp.bfloat16)

def reference(signal, filter_raw, cotangent, block_mask):
    tables = make_tables()
    factor = 1.0 / (NB * BLK * math.sqrt(SEQ))
    mask_blocks = block_mask.astype(jnp.bfloat16)[:, :, None]

    def channel(inputs):
        signal_row, filter_row, grad_row = inputs
        masked = signal_row.reshape(BATCH, RB, BLK) * mask_blocks
        signal_real, signal_imag = forward_transform(masked, tables)
        filter_real, filter_imag = forward_transform(filter_row.reshape(1, RB, BLK), tables)
        grad_real, grad_imag = forward_transform(grad_row.reshape(BATCH, RB, BLK), tables)
        out_real = signal_real * filter_real - signal_imag * filter_imag
        out_imag = signal_real * filter_imag + signal_imag * filter_real
        input_real = grad_real * filter_real + grad_imag * filter_imag
        input_imag = grad_imag * filter_real - grad_real * filter_imag
        weight_real = lax.optimization_barrier(jnp.sum(grad_real * signal_real + grad_imag * signal_imag, axis=0, keepdims=True))
        weight_imag = lax.optimization_barrier(jnp.sum(grad_imag * signal_real - grad_real * signal_imag, axis=0, keepdims=True))
        conv_rows = inverse_transform(out_real, out_imag, factor, tables)
        input_rows = inverse_transform(input_real, input_imag, factor, tables) * mask_blocks
        weight_rows = inverse_transform(weight_real, weight_imag, factor, tables)
        return (conv_rows.reshape(BATCH, SEQ), input_rows.reshape(BATCH, SEQ), weight_rows.reshape(SEQ))
    outputs = lax.map(channel, (jnp.transpose(signal, (2, 0, 1)), jnp.transpose(filter_raw, (1, 0)), jnp.transpose(cotangent, (2, 0, 1))))
    return (jnp.transpose(outputs[0], (1, 2, 0)), jnp.transpose(outputs[1], (1, 2, 0)), jnp.transpose(outputs[2], (1, 0)))
```

```python
import functools
import math

import jax
import jax.numpy as jnp
import numpy as np
from jax import lax
from jax.experimental import pallas as pl
from jax.experimental.pallas import tpu as pltpu
from jax.sharding import PartitionSpec as P

LANES = 128
ROWS = 8
SLICES = 3
PAD = 16


def make_tables(all_rows):
    full = 2 * all_rows
    period = full * LANES
    kept = all_rows + 1
    height = -(-kept // (SLICES * PAD)) * PAD
    ids = np.arange(SLICES * height)
    valid = (ids < kept).astype(np.float64)
    outer = 2.0 * np.pi / full * ((ids[:, None] * np.arange(all_rows)[None, :]) % full)
    cos_outer = (np.cos(outer) * valid[:, None]).reshape(SLICES, height, all_rows)
    sin_outer = (np.sin(outer) * valid[:, None]).reshape(SLICES, height, all_rows)
    first = np.concatenate([cos_outer, -sin_outer], axis=1)
    turn = 2.0 * np.pi / period * ((ids[:, None] * np.arange(LANES)[None, :]) % period)
    twist = np.stack([np.cos(turn), np.sin(turn)]).reshape(2, SLICES, height, LANES)
    weight = np.where((ids == 0) | (ids == all_rows), 1.0, 2.0) * valid
    back = np.concatenate([cos_outer, -sin_outer], axis=1)
    back = back * np.concatenate([weight.reshape(SLICES, height, 1)] * 2, axis=1)
    back = back.reshape(SLICES * 2 * height, all_rows).T
    inner = 2.0 * np.pi / LANES * ((np.arange(LANES)[:, None] * np.arange(LANES)[None, :]) % LANES)
    cos_in, sin_in = np.cos(inner), np.sin(inner)
    forward_in = np.block([[cos_in, -sin_in], [sin_in, cos_in]])
    inverse_in = np.block([[cos_in, sin_in], [-sin_in, cos_in]])
    low = lambda table: jnp.asarray(table.astype(np.float32), jnp.bfloat16)
    return (
        low(first),
        jnp.asarray(twist.astype(np.float32)),
        low(forward_in),
        low(inverse_in),
        low(back),
    )


def dot(left, right):
    return jnp.dot(left, right, preferred_element_type=jnp.float32)


def turn_over(left, right):
    return lax.dot_general(left, right, (((1,), (1,)), ((), ())), preferred_element_type=jnp.float32)


def gather_body(mask_ref, unit_ref, sig_ref, cot_ref, fil_ref, pair_ref, solo_ref, hold):
    unit = unit_ref[...]

    def flipped(ref):
        out = turn_over(unit, ref[...])
        for row in range(ROWS):
            hold[pl.ds(row, LANES, stride=ROWS), :] = out[:, row * LANES : (row + 1) * LANES]
        return hold[...].reshape(LANES, ROWS, LANES)

    keep = mask_ref[0, 0].astype(jnp.float32)
    pair_ref[:, :ROWS, :] = (flipped(sig_ref) * keep).astype(jnp.bfloat16)
    pair_ref[:, ROWS:, :] = flipped(cot_ref).astype(jnp.bfloat16)
    solo_ref[...] = flipped(fil_ref).astype(jnp.bfloat16)


def to_channels(block_mask, unit, signal, cotangent, filter_raw):
    tokens, channels = filter_raw.shape
    column = pl.BlockSpec((tokens, LANES), lambda i: (0, i))
    return pl.pallas_call(
        gather_body,
        grid=(channels // LANES,),
        in_specs=[
            pl.BlockSpec(memory_space=pltpu.SMEM),
            pl.BlockSpec((LANES, LANES), lambda i: (0, 0)),
            column,
            column,
            column,
        ],
        out_specs=[
            pl.BlockSpec((LANES, 2 * ROWS, LANES), lambda i: (i, 0, 0)),
            pl.BlockSpec((LANES, ROWS, LANES), lambda i: (i, 0, 0)),
        ],
        out_shape=[
            jax.ShapeDtypeStruct((channels, 2 * ROWS, LANES), jnp.bfloat16),
            jax.ShapeDtypeStruct((channels, ROWS, LANES), jnp.bfloat16),
        ],
        scratch_shapes=[pltpu.VMEM((LANES * ROWS, LANES), jnp.float32)],
        name="to_channels",
    )(block_mask, unit, signal, cotangent, filter_raw)


def scatter_body(mask_ref, unit_ref, pair_ref, solo_ref, out_ref, grad_ref, fil_ref, hold, lone):
    unit = unit_ref[...]
    hold[...] = pair_ref[...].astype(jnp.float32).reshape(LANES * 2 * ROWS, LANES)
    lone[...] = solo_ref[...].astype(jnp.float32).reshape(LANES * ROWS, LANES)
    keep = mask_ref[0, 0].astype(jnp.float32)

    def turned(ref, start, stride):
        rows = ref[pl.ds(start, LANES, stride=stride), :].astype(jnp.bfloat16)
        return turn_over(unit, rows)

    for row in range(ROWS):
        here = slice(row * LANES, (row + 1) * LANES)
        out_ref[here, :] = turned(hold, row, 2 * ROWS).astype(jnp.bfloat16)
        grad_ref[here, :] = (turned(hold, ROWS + row, 2 * ROWS) * keep).astype(jnp.bfloat16)
        fil_ref[here, :] = turned(lone, row, ROWS).astype(jnp.bfloat16)


def to_tokens(block_mask, unit, pair, solo):
    channels = solo.shape[0]
    tokens = ROWS * LANES
    column = pl.BlockSpec((tokens, LANES), lambda i: (0, i))
    return pl.pallas_call(
        scatter_body,
        grid=(channels // LANES,),
        in_specs=[
            pl.BlockSpec(memory_space=pltpu.SMEM),
            pl.BlockSpec((LANES, LANES), lambda i: (0, 0)),
            pl.BlockSpec((LANES, 2 * ROWS, LANES), lambda i: (i, 0, 0)),
            pl.BlockSpec((LANES, ROWS, LANES), lambda i: (i, 0, 0)),
        ],
        out_specs=[column, column, column],
        out_shape=[jax.ShapeDtypeStruct((tokens, channels), jnp.bfloat16)] * 3,
        scratch_shapes=[
            pltpu.VMEM((LANES * 2 * ROWS, LANES), jnp.float32),
            pltpu.VMEM((LANES * ROWS, LANES), jnp.float32),
        ],
        name="to_tokens",
    )(block_mask, unit, pair, solo)


def lane(index):
    return slice(index * LANES, (index + 1) * LANES)


def forward_slice(step, columns, rows_ref, first_ref, twist_ref, inner_ref):
    height = twist_ref.shape[2]
    cos, sin = twist_ref[0, step], twist_ref[1, step]
    mixed = dot(first_ref[step], rows_ref[...])
    spectra = []
    for column in range(columns):
        real, imag = mixed[:height, lane(column)], mixed[height:, lane(column)]
        turned = jnp.concatenate([real * cos + imag * sin, imag * cos - real * sin], axis=1)
        spectra.append(dot(turned.astype(jnp.bfloat16), inner_ref[...]))
    return spectra


def split(pair):
    return pair[:, :LANES], pair[:, LANES:]


def filter_spectrum(count, rows_ref, spec_ref, first_ref, twist_ref, inner_ref):
    def step_body(step, carry):
        spectra = forward_slice(step, count, rows_ref, first_ref, twist_ref, inner_ref)
        for index, spectrum in enumerate(spectra):
            spec_ref[index, step] = spectrum
        return carry

    lax.fori_loop(0, SLICES, step_body, 0)


def convolve(count, rows_ref, spec_ref, back_rows, tables):
    first_ref, twist_ref, inner_ref, outer_ref = tables
    height = twist_ref.shape[2]

    def step_body(step, carry):
        spectra = forward_slice(step, 2 * count, rows_ref, first_ref, twist_ref, inner_ref)
        cos, sin = twist_ref[0, step], twist_ref[1, step]
        for index in range(count):
            sig_r, sig_i = split(spectra[index])
            cot_r, cot_i = split(spectra[count + index])
            fil_r, fil_i = split(spec_ref[index, step])
            products = (
                (sig_r * fil_r - sig_i * fil_i, sig_r * fil_i + sig_i * fil_r),
                (cot_r * fil_r + cot_i * fil_i, cot_i * fil_r - cot_r * fil_i),
                (cot_r * sig_r + cot_i * sig_i, cot_i * sig_r - cot_r * sig_i),
            )
            for which, product in enumerate(products):
                low = jnp.concatenate(product, axis=1).astype(jnp.bfloat16)
                real, imag = split(dot(low, outer_ref[...]))
                column = lane(3 * index + which)
                back_rows[step, :height, column] = (real * cos - imag * sin).astype(jnp.bfloat16)
                back_rows[step, height:, column] = (imag * cos + real * sin).astype(jnp.bfloat16)
        return carry

    lax.fori_loop(0, SLICES, step_body, 0)


def finish(index, factor, back_rows, back_ref):
    depth = back_ref.shape[1]
    columns = slice(3 * index * LANES, 3 * (index + 1) * LANES)
    result = dot(back_ref[...], back_rows[:, :, columns].reshape(depth, 3 * LANES)) * factor
    blocks = result.shape[0] // ROWS
    return [result[:, lane(which)].reshape(blocks, ROWS, LANES) for which in range(3)]


LONG = 8
SHORT = 4
CORES = 2
HALVES = 2


def zigzag(step):
    return LONG + lax.div(step + 1, 2) * (1 - 2 * lax.rem(step, 2))


def partner(place, step):
    mixed = lax.rem(step * 27, LONG * SHORT * CORES)
    z = lax.rem(lax.div(place, SHORT * CORES) + zigzag(lax.rem(mixed, LONG)), LONG)
    y = lax.rem(lax.div(place, CORES) + lax.div(mixed, LONG), SHORT)
    core = lax.rem(place + lax.div(mixed, LONG * SHORT), CORES)
    return (z * SHORT + y) * CORES + core


def partner_chip(place, step):
    mixed = lax.rem(step * 11, LONG * SHORT)
    z = lax.rem(lax.div(place, SHORT * CORES) + zigzag(lax.rem(mixed, LONG)), LONG)
    y = lax.rem(lax.div(place, CORES) + lax.div(mixed, LONG), SHORT)
    return z * SHORT + y


def exchange_body(factor, pair_ref, solo_ref, *refs):
    table_refs, refs = refs[:5], refs[5:]
    pair_out, fil_out = refs[:2]
    tables = refs[2:7]
    pair_in, fil_in, rows, fil_rows, spec, back_rows, pair_done, part, parts, summed = refs[7:17]
    (table_sem, pair_sem, fil_sem, out_sem, part_sem, piece_sem, share_sem, sent_pair, sent_fil, sent_near,
     sent_fil_dp, sent_part, sent_out, sent_piece, sent_share) = refs[17:]
    peers, _, count = pair_ref.shape[:3]
    replicas = lax.axis_size("dp")
    place = lax.axis_index("seq")
    replica = lax.axis_index("dp")
    chip, core = lax.div(place, CORES), lax.rem(place, CORES)
    own_core, own_half = lax.div(replica, HALVES), lax.rem(replica, HALVES)
    sharer = core == own_core

    def remote(source, target, sent, received, **where):
        return pltpu.make_async_remote_copy(
            src_ref=source, dst_ref=target, send_sem=sent, recv_sem=received,
            device_id=where, device_id_type=pl.DeviceIdType.MESH,
        )

    def settle(like, sem):
        pltpu.make_async_copy(like, like, sem).wait()

    loads = [
        pltpu.make_async_copy(source, target, table_sem.at[index])
        for index, (source, target) in enumerate(zip(table_refs, tables))
    ]
    for load in loads:
        load.start()

    barrier = pltpu.get_barrier_semaphore()

    def greet(step, carry):
        pl.semaphore_signal(
            barrier, 1, device_id={"seq": partner(place, step)}, device_id_type=pl.DeviceIdType.MESH
        )
        return carry

    def greet_replica(step, carry):
        pl.semaphore_signal(
            barrier, 1, device_id={"dp": lax.rem(replica + step, replicas)}, device_id_type=pl.DeviceIdType.MESH
        )
        return carry

    lax.fori_loop(1, peers, greet, 0)
    lax.fori_loop(1, replicas, greet_replica, 0)
    pl.semaphore_wait(barrier, peers - 1 + replicas - 1)

    def filter_copy(to_chip):
        to = to_chip * CORES + own_core
        return remote(
            solo_ref.at[to, own_half], fil_in.at[own_half, place], sent_fil, fil_sem.at[own_half], seq=to
        )

    def near_copy():
        to = chip * CORES + own_core
        return remote(
            solo_ref.at[to, own_half], fil_in.at[own_half, place], sent_near, fil_sem.at[own_half], seq=to
        )

    def send_filter(step, carry):
        filter_copy(partner_chip(place, step)).start()
        return carry

    lax.fori_loop(1, peers // CORES, send_filter, 0)

    @pl.when(sharer)
    def _():
        pltpu.make_async_copy(
            solo_ref.at[place, own_half], fil_in.at[own_half, place], fil_sem.at[own_half]
        ).start()

    @pl.when(jnp.logical_not(sharer))
    def _():
        near_copy().start()

    def send_pairs(half):
        pltpu.make_async_copy(pair_ref.at[place, half], pair_in.at[half, place], pair_sem.at[half]).start()

        def send(step, carry):
            to = partner(place, step)
            remote(
                pair_ref.at[to, half], pair_in.at[half, place], sent_pair, pair_sem.at[half], seq=to
            ).start()
            return carry

        lax.fori_loop(1, peers, send, 0)

    send_pairs(0)

    @pl.when(sharer)
    def _():
        settle(fil_in.at[own_half], fil_sem.at[own_half])

        def share(step, carry):
            remote(
                fil_in.at[own_half], fil_in.at[own_half], sent_fil_dp, fil_sem.at[own_half],
                dp=lax.rem(replica + step, replicas),
            ).start()
            return carry

        lax.fori_loop(1, replicas, share, 0)

    send_pairs(1)

    for half in range(HALVES):
        @pl.when(replica != core * HALVES + half)
        def _():
            settle(fil_in.at[half], fil_sem.at[half])

    for load in loads:
        load.wait()
    first_ref, twist_ref, inner_ref, outer_ref, back_ref = tables
    height = peers * ROWS
    for half in range(HALVES):
        for index in range(count):
            alone = fil_in[half, :, index].astype(jnp.float32)
            fil_rows[:, lane(index)] = alone.reshape(height, LANES).astype(jnp.bfloat16)
        filter_spectrum(count, fil_rows, spec.at[half], first_ref, twist_ref, inner_ref)

    def transform(half):
        for index in range(count):
            both = pair_in[half, :, index].astype(jnp.float32)
            rows[:, lane(index)] = both[:, :ROWS].reshape(height, LANES).astype(jnp.bfloat16)
            rows[:, lane(count + index)] = both[:, ROWS:].reshape(height, LANES).astype(jnp.bfloat16)
        convolve(count, rows, spec.at[half], back_rows, (first_ref, twist_ref, inner_ref, outer_ref))
        for index in range(count):
            conv, grad, weight = finish(index, factor, back_rows, back_ref)
            pair_done[half, :, index] = jnp.concatenate([conv, grad], axis=1).astype(jnp.bfloat16)
            part[half, :, index] = weight.astype(jnp.bfloat16)

    def send_part(half):
        owner = core * HALVES + half

        @pl.when(replica != owner)
        def _():
            slot = lax.rem(replica - owner + replicas, replicas) - 1
            remote(part.at[half], parts.at[slot], sent_part.at[half], part_sem, dp=owner).start()

    def send_done(half):
        pltpu.make_async_copy(pair_done.at[half, place], pair_out.at[place, half], out_sem).start()

        def send(step, carry):
            to = partner(place, step)
            remote(pair_done.at[half, to], pair_out.at[place, half], sent_out, out_sem, seq=to).start()
            return carry

        lax.fori_loop(1, peers, send, 0)

    def collect(half):
        @pl.when(replica == core * HALVES + half)
        def _():
            settle(parts, part_sem)

            def add(block, carry):
                here = pl.ds(block * ROWS, ROWS)
                total = part[half, here].astype(jnp.float32)
                for slot in range(parts.shape[0]):
                    total = total + parts[slot, here].astype(jnp.float32)
                summed[here] = total.astype(jnp.bfloat16)
                return carry

            lax.fori_loop(0, peers // ROWS, add, 0)
            pltpu.make_async_copy(summed.at[place], fil_out.at[chip, replica], piece_sem).start()

            def send(step, carry):
                to = partner(place, step)
                remote(summed.at[to], fil_out.at[chip, replica], sent_piece, piece_sem, seq=to).start()
                return carry

            lax.fori_loop(1, peers, send, 0)

    settle(pair_in.at[0], pair_sem.at[0])
    transform(0)
    send_part(0)
    send_done(0)
    settle(pair_in.at[1], pair_sem.at[1])
    collect(0)
    transform(1)
    send_part(1)
    collect(1)
    send_done(1)

    settle(summed.at[pl.ds(0, peers // CORES)], piece_sem)

    def share_sum(step, carry):
        remote(
            fil_out.at[:, replica], fil_out.at[:, replica], sent_share, share_sem,
            dp=lax.rem(replica + step, replicas),
        ).start()
        return carry

    lax.fori_loop(1, replicas, share_sum, 0)
    shares = fil_out.at[pl.ds(0, (replicas - 1) * peers // CORES // replicas)]
    settle(shares, share_sem)
    settle(pair_out, out_sem)
    settle(pair_ref.at[pl.ds(0, peers - 1)], sent_pair)
    settle(solo_ref.at[pl.ds(0, peers // CORES - 1), 0], sent_fil)

    @pl.when(sharer)
    def _():
        settle(parts, sent_fil_dp)
        settle(summed.at[pl.ds(0, peers - 1)], sent_piece)

    @pl.when(jnp.logical_not(sharer))
    def _():
        settle(summed.at[0], sent_near)

    for half in range(HALVES):
        @pl.when(replica != core * HALVES + half)
        def _():
            settle(part.at[half], sent_part.at[half])

    settle(pair_done.at[:, pl.ds(0, peers - 1)], sent_out)
    settle(shares, sent_share)


def exchange(pair, solo, tables, factor):
    peers, halves, count = pair.shape[:3]
    height = tables[1].shape[2]
    replicas = lax.axis_size("dp")
    whole = pl.BlockSpec(memory_space=pltpu.VMEM)
    anywhere = pl.BlockSpec(memory_space=pl.ANY)
    low = jnp.bfloat16
    tile, half_tile = (count, 2 * ROWS, LANES), (count, ROWS, LANES)
    dma = pltpu.SemaphoreType.DMA
    return pl.pallas_call(
        functools.partial(exchange_body, factor),
        in_specs=[anywhere] * 7,
        out_specs=[whole] * 2,
        out_shape=[
            jax.ShapeDtypeStruct(pair.shape, low),
            jax.ShapeDtypeStruct((peers // CORES, CORES * HALVES) + half_tile, low),
        ],
        scratch_shapes=[pltpu.VMEM(table.shape, table.dtype) for table in tables]
        + [
            pltpu.VMEM((halves, peers) + tile, low),
            pltpu.VMEM((halves, peers) + half_tile, low),
            pltpu.VMEM((peers * ROWS, 2 * count * LANES), low),
            pltpu.VMEM((peers * ROWS, count * LANES), low),
            pltpu.VMEM((halves, count, SLICES, height, 2 * LANES), jnp.float32),
            pltpu.VMEM((SLICES, 2 * height, 3 * count * LANES), low),
            pltpu.VMEM((halves, peers) + tile, low),
            pltpu.VMEM((halves, peers) + half_tile, low),
            pltpu.VMEM((replicas - 1, peers) + half_tile, low),
            pltpu.VMEM((peers,) + half_tile, low),
        ]
        + [dma((len(tables),)), dma((halves,)), dma((halves,)), dma, dma, dma, dma, dma, dma, dma, dma,
           dma((halves,)), dma, dma, dma],
        compiler_params=pltpu.CompilerParams(collective_id=0, has_side_effects=True),
        name="exchange",
    )(pair, solo, *tables)


def per_device(signal, filter_raw, cotangent, block_mask):
    tokens, channels = filter_raw.shape
    peers = lax.axis_size("seq")
    own = channels // peers
    tables = make_tables(peers * tokens // LANES)
    total = peers * tokens
    factor = 1.0 / (2 * total * math.sqrt(total))
    unit = jnp.asarray(np.eye(LANES, dtype=np.float32), jnp.bfloat16)
    pair, solo = to_channels(block_mask, unit, signal[0], cotangent[0], filter_raw)
    count = own // HALVES
    pair, solo = exchange(
        pair.reshape(peers, HALVES, count, 2 * ROWS, LANES),
        solo.reshape(peers, HALVES, count, ROWS, LANES),
        tables,
        factor,
    )
    conv, grad, weight = to_tokens(
        block_mask, unit, pair.reshape(channels, 2 * ROWS, LANES), solo.reshape(channels, ROWS, LANES)
    )
    return conv[None], grad[None], weight


def solution(mesh):
    placed = (P("dp", "seq", None), P("seq", None), P("dp", "seq", None), P("dp", "seq"))
    return jax.shard_map(
        per_device,
        mesh=mesh,
        in_specs=placed,
        out_specs=(P("dp", "seq", None), P("dp", "seq", None), P("seq", None)),
        check_vma=False,
    )
```

```python
import functools
import math

import jax
import jax.numpy as jnp
import numpy as np
from jax import lax
from jax.experimental import pallas as pl
from jax.experimental.pallas import tpu as pltpu
from jax.sharding import PartitionSpec as P

LANES = 128
ROWS = 8
SLICES = 3
PAD = 16


def make_tables(all_rows):
    full = 2 * all_rows
    period = full * LANES
    kept = all_rows + 1
    height = -(-kept // (SLICES * PAD)) * PAD
    ids = np.arange(SLICES * height)
    valid = (ids < kept).astype(np.float64)
    outer = 2.0 * np.pi / full * ((ids[:, None] * np.arange(all_rows)[None, :]) % full)
    cos_outer = (np.cos(outer) * valid[:, None]).reshape(SLICES, height, all_rows)
    sin_outer = (np.sin(outer) * valid[:, None]).reshape(SLICES, height, all_rows)
    first = np.concatenate([cos_outer, -sin_outer], axis=1)
    turn = 2.0 * np.pi / period * ((ids[:, None] * np.arange(LANES)[None, :]) % period)
    twist = np.stack([np.cos(turn), np.sin(turn)]).reshape(2, SLICES, height, LANES)
    weight = np.where((ids == 0) | (ids == all_rows), 1.0, 2.0) * valid
    back = np.concatenate([cos_outer, -sin_outer], axis=1)
    back = back * np.concatenate([weight.reshape(SLICES, height, 1)] * 2, axis=1)
    back = back.reshape(SLICES * 2 * height, all_rows).T
    inner = 2.0 * np.pi / LANES * ((np.arange(LANES)[:, None] * np.arange(LANES)[None, :]) % LANES)
    cos_in, sin_in = np.cos(inner), np.sin(inner)
    forward_in = np.block([[cos_in, -sin_in], [sin_in, cos_in]])
    inverse_in = np.block([[cos_in, sin_in], [-sin_in, cos_in]])
    low = lambda table: jnp.asarray(table.astype(np.float32), jnp.bfloat16)
    return (
        low(first),
        jnp.asarray(twist.astype(np.float32)),
        low(forward_in),
        low(inverse_in),
        low(back),
    )


def dot(left, right):
    return jnp.dot(left, right, preferred_element_type=jnp.float32)


def turn_over(left, right):
    return lax.dot_general(left, right, (((1,), (1,)), ((), ())), preferred_element_type=jnp.float32)


def scatter_body(mask_ref, unit_ref, pair_ref, solo_ref, out_ref, grad_ref, fil_ref, hold, lone):
    unit = unit_ref[...]
    hold[...] = pair_ref[...].astype(jnp.float32).reshape(LANES * 2 * ROWS, LANES)
    lone[...] = solo_ref[...].astype(jnp.float32).reshape(LANES * ROWS, LANES)
    keep = mask_ref[0, 0].astype(jnp.float32)

    def turned(ref, start, stride):
        rows = ref[pl.ds(start, LANES, stride=stride), :].astype(jnp.bfloat16)
        return turn_over(unit, rows)

    for row in range(ROWS):
        here = slice(row * LANES, (row + 1) * LANES)
        out_ref[here, :] = turned(hold, row, 2 * ROWS).astype(jnp.bfloat16)
        grad_ref[here, :] = (turned(hold, ROWS + row, 2 * ROWS) * keep).astype(jnp.bfloat16)
        fil_ref[here, :] = turned(lone, row, ROWS).astype(jnp.bfloat16)


def to_tokens(block_mask, unit, pair, solo):
    channels = solo.shape[0]
    tokens = ROWS * LANES
    column = pl.BlockSpec((tokens, LANES), lambda i: (0, i))
    return pl.pallas_call(
        scatter_body,
        grid=(channels // LANES,),
        in_specs=[
            pl.BlockSpec(memory_space=pltpu.SMEM),
            pl.BlockSpec((LANES, LANES), lambda i: (0, 0)),
            pl.BlockSpec((LANES, 2 * ROWS, LANES), lambda i: (i, 0, 0)),
            pl.BlockSpec((LANES, ROWS, LANES), lambda i: (i, 0, 0)),
        ],
        out_specs=[column, column, column],
        out_shape=[jax.ShapeDtypeStruct((tokens, channels), jnp.bfloat16)] * 3,
        scratch_shapes=[
            pltpu.VMEM((LANES * 2 * ROWS, LANES), jnp.float32),
            pltpu.VMEM((LANES * ROWS, LANES), jnp.float32),
        ],
        name="to_tokens",
    )(block_mask, unit, pair, solo)


def lane(index):
    return slice(index * LANES, (index + 1) * LANES)


def forward_slice(step, columns, rows_ref, first_ref, twist_ref, inner_ref):
    height = twist_ref.shape[2]
    cos, sin = twist_ref[0, step], twist_ref[1, step]
    mixed = dot(first_ref[step], rows_ref[...])
    spectra = []
    for column in range(columns):
        real, imag = mixed[:height, lane(column)], mixed[height:, lane(column)]
        turned = jnp.concatenate([real * cos + imag * sin, imag * cos - real * sin], axis=1)
        spectra.append(dot(turned.astype(jnp.bfloat16), inner_ref[...]))
    return spectra


def split(pair):
    return pair[:, :LANES], pair[:, LANES:]


def filter_spectrum(count, rows_ref, spec_ref, first_ref, twist_ref, inner_ref):
    def step_body(step, carry):
        spectra = forward_slice(step, count, rows_ref, first_ref, twist_ref, inner_ref)
        for index, spectrum in enumerate(spectra):
            spec_ref[index, step] = spectrum
        return carry

    lax.fori_loop(0, SLICES, step_body, 0)


def convolve(count, rows_ref, spec_ref, back_rows, tables):
    first_ref, twist_ref, inner_ref, outer_ref = tables
    height = twist_ref.shape[2]

    def step_body(step, carry):
        spectra = forward_slice(step, 2 * count, rows_ref, first_ref, twist_ref, inner_ref)
        cos, sin = twist_ref[0, step], twist_ref[1, step]
        for index in range(count):
            sig_r, sig_i = split(spectra[index])
            cot_r, cot_i = split(spectra[count + index])
            fil_r, fil_i = split(spec_ref[index, step])
            products = (
                (sig_r * fil_r - sig_i * fil_i, sig_r * fil_i + sig_i * fil_r),
                (cot_r * fil_r + cot_i * fil_i, cot_i * fil_r - cot_r * fil_i),
                (cot_r * sig_r + cot_i * sig_i, cot_i * sig_r - cot_r * sig_i),
            )
            for which, product in enumerate(products):
                low = jnp.concatenate(product, axis=1).astype(jnp.bfloat16)
                real, imag = split(dot(low, outer_ref[...]))
                column = lane(3 * index + which)
                back_rows[step, :height, column] = (real * cos - imag * sin).astype(jnp.bfloat16)
                back_rows[step, height:, column] = (imag * cos + real * sin).astype(jnp.bfloat16)
        return carry

    lax.fori_loop(0, SLICES, step_body, 0)


def finish(index, factor, back_rows, back_ref):
    depth = back_ref.shape[1]
    columns = slice(3 * index * LANES, 3 * (index + 1) * LANES)
    result = dot(back_ref[...], back_rows[:, :, columns].reshape(depth, 3 * LANES)) * factor
    blocks = result.shape[0] // ROWS
    return [result[:, lane(which)].reshape(blocks, ROWS, LANES) for which in range(3)]


LONG = 8
SHORT = 4
CORES = 2
HALVES = 2


ZIGZAG = (0, -1, 1, -2, 2, -3, 3, -4)


def wrap(value, size):
    return jnp.where(value >= size, value - size, value)


def each_partner(place, visit):
    z, y, core = lax.div(place, SHORT * CORES), lax.rem(lax.div(place, CORES), SHORT), lax.rem(place, CORES)
    bases = [wrap(z + shift % LONG, LONG) * (SHORT * CORES) for shift in ZIGZAG]
    sides = (core, 1 - core)

    def body(turn, carry):
        first = wrap(y + turn, SHORT)
        rows = [wrap(first + shift, SHORT) * CORES for shift in range(SHORT)]
        for swap in range(CORES):
            for index, base in enumerate(bases):
                to = base + rows[index % SHORT] + sides[(swap + index // SHORT) % CORES]
                if swap == 0 and index == 0:

                    @pl.when(turn > 0)
                    def _():
                        visit(to)
                else:
                    visit(to)
        return carry

    lax.fori_loop(0, SHORT, body, 0)


def each_chip(place, visit):
    z, y = lax.div(place, SHORT * CORES), lax.rem(lax.div(place, CORES), SHORT)
    bases = [wrap(z + shift % LONG, LONG) * SHORT for shift in ZIGZAG]

    def body(turn, carry):
        first = wrap(y + turn, SHORT)
        rows = [wrap(first + shift, SHORT) for shift in range(SHORT)]
        for index, base in enumerate(bases):
            to = base + rows[index % SHORT]
            if index == 0:

                @pl.when(turn > 0)
                def _():
                    visit(to)
            else:
                visit(to)
        return carry

    lax.fori_loop(0, SHORT, body, 0)


def flip(unit, tokens_ref, column, hold):
    across = turn_over(unit, tokens_ref[:, lane(column)])
    for row in range(ROWS):
        hold[pl.ds(row, LANES, stride=ROWS), :] = across[:, lane(row)]
    return hold[...].reshape(LANES, ROWS, LANES)


def exchange_body(factor, count, mask_ref, unit_ref, *refs):
    token_refs, table_refs, refs = refs[:3], refs[3:8], refs[8:]
    pair_out, fil_out = refs[:2]
    tables = refs[2:7]
    (fil_tokens, sig_tokens, cot_tokens, hold, pair_ready, fil_ready, pair_in, fil_in, rows, fil_rows, spec,
     back_rows, pair_done, part, parts, summed) = refs[7:23]
    (token_sem, table_sem, pair_sem, fil_sem, out_sem, part_sem, piece_sem, share_sem, sent_pair, sent_fil, sent_near,
     sent_fil_dp, sent_part, sent_out, sent_piece, sent_share) = refs[23:]
    peers = lax.axis_size("seq")
    replicas = lax.axis_size("dp")
    place = lax.axis_index("seq")
    replica = lax.axis_index("dp")
    chip, core = lax.div(place, CORES), lax.rem(place, CORES)
    own_core, own_half = lax.div(replica, HALVES), lax.rem(replica, HALVES)
    sharer = core == own_core

    def remote(source, target, sent, received, **where):
        return pltpu.make_async_remote_copy(
            src_ref=source, dst_ref=target, send_sem=sent, recv_sem=received,
            device_id=where, device_id_type=pl.DeviceIdType.MESH,
        )

    def settle(like, sem):
        pltpu.make_async_copy(like, like, sem).wait()

    inputs = [
        pltpu.make_async_copy(source, target, token_sem.at[index])
        for index, (source, target) in enumerate(zip(token_refs, (fil_tokens, sig_tokens, cot_tokens)))
    ]
    for load in inputs:
        load.start()
    loads = [
        pltpu.make_async_copy(source, target, table_sem.at[index])
        for index, (source, target) in enumerate(zip(table_refs, tables))
    ]
    barrier = pltpu.get_barrier_semaphore()

    def greet(**where):
        pl.semaphore_signal(barrier, 1, device_id=where, device_id_type=pl.DeviceIdType.MESH)

    def greet_replica(step, carry):
        greet(dp=lax.rem(replica + step, replicas))
        return carry

    each_partner(place, lambda to: greet(seq=to))
    lax.fori_loop(1, replicas, greet_replica, 0)

    unit = unit_ref[...]
    columns = fil_tokens.shape[1] // LANES
    inputs[0].wait()
    for column in range(columns):
        fil_ready[lane(column)] = flip(unit, fil_tokens, column, hold).astype(jnp.bfloat16)
    inputs[1].wait()
    inputs[2].wait()
    keep = mask_ref[0, 0].astype(jnp.float32)
    for column in range(columns):
        sig = flip(unit, sig_tokens, column, hold) * keep
        cot = flip(unit, cot_tokens, column, hold)
        pair_ready[lane(column)] = jnp.concatenate([sig, cot], axis=1).astype(jnp.bfloat16)

    def channels(to, half):
        return pl.ds((to * HALVES + half) * count, count)

    pl.semaphore_wait(barrier, peers - 1 + replicas - 1)
    for load in loads:
        load.start()

    def filter_copy(to, sent):
        return remote(
            fil_ready.at[channels(to, own_half)], fil_in.at[own_half, place], sent, fil_sem.at[own_half], seq=to
        )

    each_chip(place, lambda to: filter_copy(to * CORES + own_core, sent_fil).start())

    @pl.when(sharer)
    def _():
        pltpu.make_async_copy(
            fil_ready.at[channels(place, own_half)], fil_in.at[own_half, place], fil_sem.at[own_half]
        ).start()

    @pl.when(jnp.logical_not(sharer))
    def _():
        filter_copy(chip * CORES + own_core, sent_near).start()

    def send_pairs(half):
        pltpu.make_async_copy(
            pair_ready.at[channels(place, half)], pair_in.at[half, place], pair_sem.at[half]
        ).start()
        each_partner(place, lambda to: remote(
            pair_ready.at[channels(to, half)], pair_in.at[half, place], sent_pair, pair_sem.at[half], seq=to
        ).start())

    send_pairs(0)

    @pl.when(sharer)
    def _():
        settle(fil_in.at[own_half], fil_sem.at[own_half])

        def share(step, carry):
            remote(
                fil_in.at[own_half], fil_in.at[own_half], sent_fil_dp, fil_sem.at[own_half],
                dp=lax.rem(replica + step, replicas),
            ).start()
            return carry

        lax.fori_loop(1, replicas, share, 0)

    send_pairs(1)

    for half in range(HALVES):
        @pl.when(replica != core * HALVES + half)
        def _():
            settle(fil_in.at[half], fil_sem.at[half])

    for load in loads:
        load.wait()
    first_ref, twist_ref, inner_ref, outer_ref, back_ref = tables
    height = peers * ROWS
    for half in range(HALVES):
        for index in range(count):
            alone = fil_in[half, :, index].astype(jnp.float32)
            fil_rows[:, lane(index)] = alone.reshape(height, LANES).astype(jnp.bfloat16)
        filter_spectrum(count, fil_rows, spec.at[half], first_ref, twist_ref, inner_ref)

    def transform(half):
        for index in range(count):
            both = pair_in[half, :, index].astype(jnp.float32)
            rows[:, lane(index)] = both[:, :ROWS].reshape(height, LANES).astype(jnp.bfloat16)
            rows[:, lane(count + index)] = both[:, ROWS:].reshape(height, LANES).astype(jnp.bfloat16)
        convolve(count, rows, spec.at[half], back_rows, (first_ref, twist_ref, inner_ref, outer_ref))
        for index in range(count):
            conv, grad, weight = finish(index, factor, back_rows, back_ref)
            pair_done[half, :, index] = jnp.concatenate([conv, grad], axis=1).astype(jnp.bfloat16)
            part[half, :, index] = weight.astype(jnp.bfloat16)

    def send_part(half):
        owner = core * HALVES + half

        @pl.when(replica != owner)
        def _():
            slot = lax.rem(replica - owner + replicas, replicas) - 1
            remote(part.at[half], parts.at[slot], sent_part.at[half], part_sem, dp=owner).start()

    def send_done(half):
        pltpu.make_async_copy(pair_done.at[half, place], pair_out.at[place, half], out_sem).start()

        each_partner(place, lambda to: remote(
            pair_done.at[half, to], pair_out.at[place, half], sent_out, out_sem, seq=to
        ).start())

    def collect(half):
        @pl.when(replica == core * HALVES + half)
        def _():
            settle(parts, part_sem)

            def add(block, carry):
                here = pl.ds(block * ROWS, ROWS)
                total = part[half, here].astype(jnp.float32)
                for slot in range(parts.shape[0]):
                    total = total + parts[slot, here].astype(jnp.float32)
                summed[here] = total.astype(jnp.bfloat16)
                return carry

            lax.fori_loop(0, peers // ROWS, add, 0)
            pltpu.make_async_copy(summed.at[place], fil_out.at[chip, replica], piece_sem).start()

            each_partner(place, lambda to: remote(
                summed.at[to], fil_out.at[chip, replica], sent_piece, piece_sem, seq=to
            ).start())

    settle(pair_in.at[0], pair_sem.at[0])
    transform(0)
    send_part(0)
    send_done(0)
    settle(pair_in.at[1], pair_sem.at[1])
    collect(0)
    transform(1)
    send_part(1)
    collect(1)
    send_done(1)

    settle(summed.at[pl.ds(0, peers // CORES)], piece_sem)

    def share_sum(step, carry):
        remote(
            fil_out.at[:, replica], fil_out.at[:, replica], sent_share, share_sem,
            dp=lax.rem(replica + step, replicas),
        ).start()
        return carry

    lax.fori_loop(1, replicas, share_sum, 0)
    shares = fil_out.at[pl.ds(0, (replicas - 1) * peers // CORES // replicas)]
    settle(shares, share_sem)
    settle(pair_out, out_sem)
    settle(pair_in.at[:, pl.ds(0, peers - 1)], sent_pair)
    settle(fil_in.at[0, pl.ds(0, peers // CORES - 1)], sent_fil)

    @pl.when(sharer)
    def _():
        settle(parts, sent_fil_dp)
        settle(summed.at[pl.ds(0, peers - 1)], sent_piece)

    @pl.when(jnp.logical_not(sharer))
    def _():
        settle(summed.at[0], sent_near)

    for half in range(HALVES):
        @pl.when(replica != core * HALVES + half)
        def _():
            settle(part.at[half], sent_part.at[half])

    settle(pair_done.at[:, pl.ds(0, peers - 1)], sent_out)
    settle(shares, sent_share)


def exchange(block_mask, unit, filter_raw, signal, cotangent, tables, factor):
    tokens, channels = filter_raw.shape
    peers, replicas = lax.axis_size("seq"), lax.axis_size("dp")
    count = channels // peers // HALVES
    height = tables[1].shape[2]
    whole = pl.BlockSpec(memory_space=pltpu.VMEM)
    anywhere = pl.BlockSpec(memory_space=pl.ANY)
    low = jnp.bfloat16
    tile, half_tile = (count, 2 * ROWS, LANES), (count, ROWS, LANES)
    dma = pltpu.SemaphoreType.DMA
    return pl.pallas_call(
        functools.partial(exchange_body, factor, count),
        in_specs=[pl.BlockSpec(memory_space=pltpu.SMEM), whole] + [anywhere] * 8,
        out_specs=[anywhere] * 2,
        out_shape=[
            jax.ShapeDtypeStruct((peers, HALVES) + tile, low),
            jax.ShapeDtypeStruct((peers // CORES, CORES * HALVES) + half_tile, low),
        ],
        scratch_shapes=[pltpu.VMEM(table.shape, table.dtype) for table in tables]
        + [pltpu.VMEM((tokens, channels), low)] * 3
        + [
            pltpu.VMEM((LANES * ROWS, LANES), jnp.float32),
            pltpu.VMEM((channels, 2 * ROWS, LANES), low),
            pltpu.VMEM((channels, ROWS, LANES), low),
            pltpu.VMEM((HALVES, peers) + tile, low),
            pltpu.VMEM((HALVES, peers) + half_tile, low),
            pltpu.VMEM((peers * ROWS, 2 * count * LANES), low),
            pltpu.VMEM((peers * ROWS, count * LANES), low),
            pltpu.VMEM((HALVES, count, SLICES, height, 2 * LANES), jnp.float32),
            pltpu.VMEM((SLICES, 2 * height, 3 * count * LANES), low),
            pltpu.VMEM((HALVES, peers) + tile, low),
            pltpu.VMEM((HALVES, peers) + half_tile, low),
            pltpu.VMEM((replicas - 1, peers) + half_tile, low),
            pltpu.VMEM((peers,) + half_tile, low),
        ]
        + [dma((3,)), dma((len(tables),)), dma((HALVES,)), dma((HALVES,)), dma, dma, dma, dma, dma, dma, dma, dma,
           dma((HALVES,)), dma, dma, dma],
        compiler_params=pltpu.CompilerParams(collective_id=0, has_side_effects=True),
        name="exchange",
    )(block_mask, unit, filter_raw, signal, cotangent, *tables)


def per_device(signal, filter_raw, cotangent, block_mask):
    tokens, channels = filter_raw.shape
    peers = lax.axis_size("seq")
    tables = make_tables(peers * tokens // LANES)
    total = peers * tokens
    factor = 1.0 / (2 * total * math.sqrt(total))
    unit = jnp.asarray(np.eye(LANES, dtype=np.float32), jnp.bfloat16)
    pair, solo = exchange(block_mask, unit, filter_raw, signal[0], cotangent[0], tables, factor)
    conv, grad, weight = to_tokens(
        block_mask, unit, pair.reshape(channels, 2 * ROWS, LANES), solo.reshape(channels, ROWS, LANES)
    )
    return conv[None], grad[None], weight


def solution(mesh):
    placed = (P("dp", "seq", None), P("seq", None), P("dp", "seq", None), P("dp", "seq"))
    return jax.shard_map(
        per_device,
        mesh=mesh,
        in_specs=placed,
        out_specs=(P("dp", "seq", None), P("dp", "seq", None), P("seq", None)),
        check_vma=False,
    )
```
